32 devices in a mesh: ga: 16 (over z, y, x), band: 2 (over core).
Axes of the slice: x: 2, y: 2, z: 4, core: 2. Of those that a mesh axis runs over, the one named last changes fastest.
Arguments:
- coefficients: float32 [2048, 2, 8192], P('band', None, 'ga'), may hold values from -6 to 6
- rotation: float32 [2, 2048, 32], P(None, 'band', 'ga'), may hold values from -0.125 to 0.125
- potential: float32 [64, 4096], P(None, 'ga'), may hold values from -2 to 0.5
- index_map: int32 [8192], replicated, may hold values from 0 to 262143, as said below
- counts: int32 [16], replicated, may hold values from 384 to 512, as said below
Outputs:
- applied_panel: float32 [32, 2, 32, 1024], P(('band', 'ga'))
The draws below stay inside these ranges and needn't reach their ends.
Inputs may be any that keep to these rules, and one draw needn't show every extreme that they name: counts[i] counts the live slots of index i of ga, which are its slots 0 to counts[i] - 1 of 512; the counts sum to 7168, and some index has exactly 512. `index_map`: live slots name distinct cells, and together exactly 7168 cells whose signed frequency vector has a squared length no larger than that of any cell not named (a ball about the anchor), every signed component of a live cell lying in -16 to 15; dead slots name arbitrary cells.
All inputs are finite; a program needn't handle non-finite values.
Results may differ from the reference program's by a relative error of at most 0.00008.
Values sent between devices are 32-bit elements; how exact they have to be, the bound alone decides.
A program may use at most 128 MiB of HBM per device.

```python
import jax
import jax.numpy as jnp
from jax import lax

BANDS = 2048
BOX = 64
SLOT_DEV = 512
PW_DEV = 448
NPW = 7168
PANEL = 32
N_GA = 16


def layout_draw(key):
    folded = jax.random.fold_in(key, 7)
    key_ties, key_shuffle, key_pairs, key_order, key_dead = jax.random.split(folded, 5)
    cell_count = BOX * BOX * BOX
    flat_cells = jnp.arange(cell_count, dtype=jnp.int32)
    freq_x = flat_cells // (BOX * BOX)
    freq_y = flat_cells // BOX % BOX
    freq_z = flat_cells % BOX
    freq_x = jnp.where(freq_x >= BOX // 2, freq_x - BOX, freq_x)
    freq_y = jnp.where(freq_y >= BOX // 2, freq_y - BOX, freq_y)
    freq_z = jnp.where(freq_z >= BOX // 2, freq_z - BOX, freq_z)
    squared_norm = freq_x * freq_x + freq_y * freq_y + freq_z * freq_z
    ties_rank = jax.random.permutation(key_ties, cell_count).astype(jnp.int32)
    ranking = jnp.argsort(squared_norm * cell_count + ties_rank, stable=True).astype(jnp.int32)
    ball_cells = jax.random.permutation(key_shuffle, ranking[:NPW])
    dead_mean = SLOT_DEV - PW_DEV
    pair_count = N_GA // 2
    shifts = jax.random.randint(key_pairs, (pair_count,), -dead_mean, dead_mean + 1).astype(jnp.int32)
    shifts = shifts.at[0].set(dead_mean)
    dead_slots = jnp.concatenate([dead_mean + shifts, dead_mean - shifts])
    dead_slots = jax.random.permutation(key_order, dead_slots)
    counts = (SLOT_DEV - dead_slots).astype(jnp.int32)
    offsets = jnp.cumsum(counts) - counts
    slot_ids = jnp.arange(SLOT_DEV, dtype=jnp.int32)
    slot_pos = jnp.clip(offsets[:, None] + slot_ids[None, :], 0, NPW - 1)
    live_mask = slot_ids[None, :] < counts[:, None]
    filler = jax.random.randint(key_dead, (N_GA, SLOT_DEV), 0, cell_count).astype(jnp.int32)
    index_map = jnp.where(live_mask, ball_cells[slot_pos], filler).reshape(-1).astype(jnp.int32)
    return (index_map, counts)


def draw_index_map(key, part):
    return layout_draw(key)[0]


def draw_counts(key, part):
    return layout_draw(key)[1]


def spiked(entries, rng, source, target, shards_of, factor):
    owner, partner = [(jnp.arange(entries.shape[dim]) // (entries.shape[dim] // shards_of)).reshape([-1 if axis == dim else 1 for axis in range(entries.ndim)]) for dim in (source, target)]
    chosen = jax.random.permutation(rng, shards_of)[partner]
    strong = (owner == chosen) | (owner == (partner + shards_of // 2) % shards_of)
    return jnp.where(strong, factor * entries, entries)


def level_of(own_key, extent, cuts, least, largest):
    level = 1.0
    for axis_at, shards_of in cuts:
        draws = jax.random.uniform(jax.random.fold_in(jax.random.fold_in(own_key, 6), axis_at), (shards_of,), jnp.float32, least / len(cuts), largest / len(cuts))
        level = level * jnp.repeat(jnp.exp(draws), extent[axis_at] // shards_of).reshape((-1,) + (1,) * (len(extent) - 1 - axis_at))
    return level


def normal_values(rng, extent, deviation, limit, pieces=(), held_as=jnp.bfloat16):
    values = deviation * jax.random.normal(rng, extent, jnp.float32)
    if pieces:
        values = values * level_of(rng, extent, pieces, -0.22, 0.18)
    return jnp.clip(values, -limit, limit).astype(held_as)


def noise_with(key, dims, width, limit, pieces, heavy, kind=jnp.bfloat16):
    result = width * jax.random.normal(key, dims, jnp.float32)
    if pieces:
        result = result * level_of(key, dims, pieces, -0.22, 0.18)
    return jnp.clip(spiked(result, jax.random.fold_in(key, 3), *heavy), -limit, limit).astype(kind)


def setup_inputs(seed: int = 0) -> dict:
    streams_of = jax.random.split(jax.random.key(seed), 6)
    coefficients = normal_values(streams_of[0], (BANDS, 2, SLOT_DEV * N_GA), 1.0, 6.0, ((0, 2), (2, 16)), jnp.float32)
    rotation = noise_with(streams_of[1], (2, BANDS, PANEL), (2 * BANDS) ** -0.5, 0.125, ((1, 2), (2, 16)), (1, 2, 16, 2.0), jnp.float32)
    potential = jnp.clip(-2.0 + 2.5 * jax.random.uniform(streams_of[2], (BOX, BOX * BOX), jnp.float32) ** level_of(streams_of[2], (BOX, BOX * BOX), ((1, 16),), -0.2, 0.2), -2.0, 0.5)
    index_map = draw_index_map(jax.random.fold_in(streams_of[5], 71), 0)
    counts = draw_counts(jax.random.fold_in(streams_of[5], 71), 0)
    return {"coefficients": coefficients, "rotation": rotation, "potential": potential, "index_map": index_map, "counts": counts}


def mixing(columns):
    real_cols = columns[0].T
    imag_cols = columns[1].T
    upper_rows = jnp.stack([real_cols, -imag_cols], axis=-1)
    lower_rows = jnp.stack([imag_cols, real_cols], axis=-1)
    stacked = jnp.stack([upper_rows, lower_rows], axis=1)
    return stacked.reshape(2 * real_cols.shape[0], 2 * real_cols.shape[1])


def kinetic_grid(box_edge):
    ticks_index = jnp.arange(box_edge, dtype=jnp.int32)
    signed = jnp.where(ticks_index >= box_edge // 2, ticks_index - box_edge, ticks_index).astype(jnp.float32)
    squared = signed[:, None, None] ** 2 + signed[None, :, None] ** 2 + signed[None, None, :] ** 2
    return (8.0 / (box_edge * box_edge)) * squared


def reference(coefficients, rotation, potential, index_map, counts):
    band_count = coefficients.shape[0]
    slot_total = coefficients.shape[2]
    mixer_rows = mixing(rotation)
    rotated = jnp.dot(mixer_rows, coefficients.reshape(2 * band_count, slot_total),
                      precision=lax.Precision.HIGHEST).reshape(PANEL, 2, slot_total)
    slot_ids = jnp.arange(SLOT_DEV, dtype=jnp.int32)
    live_mask = (slot_ids[None, :] < counts[:, None]).reshape(-1).astype(jnp.float32)
    kinetic = kinetic_grid(BOX)
    pot_grid = potential.reshape(BOX, BOX, BOX)
    window = BOX // 2
    window_ids = ((jnp.arange(window, dtype=jnp.int32) - window // 2) % BOX).astype(jnp.int32)

    def one_band(values):
        masked = values * live_mask[None, :]
        box_cells = jnp.zeros((2, BOX * BOX * BOX), jnp.float32).at[:, index_map].add(masked)
        grid_field = (box_cells[0] + 1j * box_cells[1]).reshape(BOX, BOX, BOX)
        real_space = jnp.fft.ifftn(grid_field)
        applied = jnp.fft.fftn(pot_grid * real_space) + kinetic * grid_field
        applied = jnp.take(applied, window_ids, axis=0)
        applied = jnp.take(applied, window_ids, axis=1)
        applied = jnp.take(applied, window_ids, axis=2)
        return jnp.stack([applied.real, applied.imag]).reshape(2, window, window * window)

    return lax.map(one_band, rotated)
```

```python
import functools
import math

import jax
import jax.numpy as jnp
import numpy as np
from jax import lax
from jax.experimental import pallas as pl
from jax.experimental.pallas import tpu as pltpu
from jax.sharding import PartitionSpec as P

F32 = jnp.float32
BF16 = jnp.bfloat16


def mixing(columns):
    real_cols = columns[0].T
    imag_cols = columns[1].T
    upper_rows = jnp.stack([real_cols, -imag_cols], axis=-1)
    lower_rows = jnp.stack([imag_cols, real_cols], axis=-1)
    stacked = jnp.stack([upper_rows, lower_rows], axis=1)
    return stacked.reshape(2 * real_cols.shape[0], 2 * real_cols.shape[1])


def split_parts(values):
    high = values.astype(BF16)
    return high, (values - high.astype(F32)).astype(BF16)


def two_parts(table):
    high = table.astype(BF16)
    low = (table - high.astype(np.float32)).astype(BF16)
    return np.stack([high, low])


def tables(box, window, radix):
    half = window // 2
    coarse = window // radix
    k_all = np.arange(box)
    k_coarse = np.arange(box // radix)
    n_signed = np.arange(window) - half
    low = np.arange(radix)
    y_phase = (radix * np.arange(coarse) - half)[:, None] * low[None, :]
    z_phase = n_signed[:, None] * k_all[None, :]
    right = y_phase[:, None, :, None] + z_phase[None, :, None, :]
    right = right.reshape(coarse * window, radix * box) % box
    x_phase = k_all[:, None] * n_signed[None, :]
    l_phase = radix * k_coarse[:, None] * low[None, :]
    left = l_phase[:, None, :, None] + x_phase[None, :, None, :]
    left = left.reshape(k_coarse.size * box, radix * window) % box
    twist = np.repeat(low[:, None] * low[None, :], box, axis=1) % box

    def pair(phase, scale=1.0):
        angle = phase * (2.0 * math.pi / box)
        return (np.stack([np.cos(angle), np.sin(angle)]) * scale).astype(np.float32)

    right_tab = two_parts(pair(right))
    left_pair = pair(left, 1.0 / box**3)
    left_tab = two_parts(left_pair)
    back_tab = two_parts((left_pair * np.float32(box**3)).transpose(0, 2, 1).copy())
    return right_tab, left_tab, back_tab, pair(twist)


def dot3(lhs, rhs, dims=((1,), (0,))):
    def one(a, b):
        return lax.dot_general(a, b, (dims, ((), ())), preferred_element_type=F32)

    return one(lhs[0], rhs[0]) + (one(lhs[0], rhs[1]) + one(lhs[1], rhs[0]))


def block(cos, sin):
    upper = jnp.concatenate([cos, sin], axis=1)
    lower = jnp.concatenate([-sin, cos], axis=1)
    return jnp.concatenate([upper, lower], axis=0)


def apply_kernel(
    box, window, radix, chunk, val_ref, row_ref, col_ref, pot_ref, right_ref, left_ref, back_ref, twist_ref, out_ref, acc
):
    coarse = window // radix
    rows = radix * window
    cols = coarse * window
    wide = radix * box
    slots = val_ref.shape[1]
    acc[...] = jnp.zeros_like(acc)

    def scatter(step, carry):
        at = pl.ds(pl.multiple_of(step * chunk, chunk), chunk)
        row_id = row_ref[:, at]
        col_id = col_ref[:, at]
        picks = lax.broadcasted_iota(jnp.int32, (rows, chunk), 0) == row_id
        onehot = jnp.where(picks, 1.0, 0.0).astype(BF16)
        hits = lax.broadcasted_iota(jnp.int32, (cols, chunk), 0) == col_id
        high, low = split_parts(val_ref[:, at])
        high, low = high.astype(F32), low.astype(F32)
        placed = [
            jnp.where(hits, part[c : c + 1, :], 0.0).astype(BF16)
            for part in (high, low)
            for c in range(2)
        ]
        acc[...] += lax.dot_general(
            onehot,
            jnp.concatenate(placed, axis=0),
            (((1,), (1,)), ((), ())),
            preferred_element_type=F32,
        )
        return carry

    lax.fori_loop(0, slots // chunk, scatter, 0)
    grid_field = acc[:, : 2 * cols] + acc[:, 2 * cols :]

    right = [block(right_ref[i, 0], right_ref[i, 1]) for i in range(2)]
    field = dot3(split_parts(grid_field), right)
    cos = twist_ref[0][:, None, :]
    sin = twist_ref[1][:, None, :]
    real = field[:, :wide].reshape(radix, window, wide)
    imag = field[:, wide:].reshape(radix, window, wide)
    turned = jnp.concatenate(
        [
            (real * cos - imag * sin).reshape(rows, wide),
            (real * sin + imag * cos).reshape(rows, wide),
        ],
        axis=0,
    )
    left = [block(left_ref[i, 0], -left_ref[i, 1]) for i in range(2)]
    space = dot3(left, split_parts(turned))
    pot = jnp.concatenate(
        [pot_ref[:, k * wide : (k + 1) * wide] for k in range(box // radix)], axis=0
    )
    space = space * jnp.concatenate([pot, pot], axis=0)
    back = [block(back_ref[i, 0], back_ref[i, 1]) for i in range(2)]
    field = dot3(back, split_parts(space))
    real = field[:rows].reshape(radix, window, wide)
    imag = field[rows:].reshape(radix, window, wide)
    turned = jnp.concatenate(
        [
            (real * cos + imag * sin).reshape(rows, wide),
            (imag * cos - real * sin).reshape(rows, wide),
        ],
        axis=1,
    )
    applied = dot3(split_parts(turned), right, ((1,), (1,)))

    half = window // 2
    row_at = lax.broadcasted_iota(jnp.int32, (rows, cols), 0)
    col_at = lax.broadcasted_iota(jnp.int32, (rows, cols), 1)
    n_x = (row_at % window - half).astype(F32)
    n_y = (col_at // window * radix + row_at // window - half).astype(F32)
    n_z = (col_at % window - half).astype(F32)
    kinetic = (8.0 / (box * box)) * (n_x * n_x + n_y * n_y + n_z * n_z)
    applied = applied + jnp.concatenate([kinetic, kinetic], axis=1) * grid_field
    for c in range(2):
        pieces = [
            applied[lo * window : (lo + 1) * window, c * cols + hi * window : c * cols + (hi + 1) * window]
            for hi in range(coarse)
            for lo in range(radix)
        ]
        out_ref[c] = jnp.concatenate(pieces, axis=1)


def apply_band(values, row_id, col_id, pot_full, window, radix, consts):
    box = pot_full.shape[0]
    slots = values.shape[1]
    chunk = math.gcd(slots, 1024)
    vmem = pl.BlockSpec(memory_space=pltpu.VMEM)
    return pl.pallas_call(
        functools.partial(apply_kernel, box, window, radix, chunk),
        out_shape=jax.ShapeDtypeStruct((2, window, window * window), F32),
        in_specs=[vmem] * 8,
        out_specs=vmem,
        scratch_shapes=[pltpu.VMEM((radix * window, 4 * (window // radix) * window), F32)],
        compiler_params=pltpu.CompilerParams(vmem_limit_bytes=60 * 1024 * 1024),
    )(values, row_id, col_id, pot_full, *consts)


def per_device(coefficients, rotation, potential, index_map, counts):
    mixer = lax.all_gather(mixing(rotation), "ga", axis=0, tiled=True)
    pot_full = lax.all_gather(potential, "ga", axis=1, tiled=True)
    band_local = coefficients.shape[0]
    slot_local = coefficients.shape[2]
    flat_coeffs = coefficients.reshape(2 * band_local, slot_local)
    box = pot_full.shape[0]
    window = box // 2
    half = window // 2
    radix = math.isqrt(box)
    assert radix * radix == box
    slots_each = index_map.shape[0] // counts.shape[0]
    slot_ids = jnp.arange(slots_each, dtype=jnp.int32)
    live = (slot_ids[None, :] < counts[:, None]).reshape(-1)
    cell_x = (index_map // (box * box) + half) % box
    cell_y = (index_map // box % box + half) % box
    cell_z = (index_map % box + half) % box
    inside = (cell_x < window) & (cell_y < window) & (cell_z < window)
    row_id = jnp.where(live & inside, cell_y % radix * window + cell_x, -1)[None]
    col_id = (cell_y // radix * window + cell_z)[None]
    consts = [jnp.asarray(t) for t in tables(box, window, radix)]

    product = jnp.dot(mixer, flat_coeffs, precision=lax.Precision.HIGH)
    panel_rows = mixer.shape[0] // 2
    summed = lax.psum_scatter(
        product.reshape(panel_rows, 2, slot_local), "band", scatter_dimension=0, tiled=True
    )
    groups = lax.axis_size("ga")
    grouped = summed.reshape(groups, summed.shape[0] // groups, 2, slot_local)
    values = lax.all_to_all(grouped, "ga", split_axis=0, concat_axis=3, tiled=True)[0]
    return jnp.stack(
        [
            apply_band(values[i], row_id, col_id, pot_full, window, radix, consts)
            for i in range(values.shape[0])
        ]
    )


def solution(mesh):
    placed = (P("band", None, "ga"), P(None, "band", "ga"), P(None, "ga"), P(), P())
    return jax.shard_map(
        per_device,
        mesh=mesh,
        in_specs=placed,
        out_specs=P(("band", "ga"), None, None, None),
        check_vma=False,
    )
```

```python
import functools
import math

import jax
import jax.numpy as jnp
import numpy as np
from jax import lax
from jax.experimental import pallas as pl
from jax.experimental.pallas import tpu as pltpu
from jax.sharding import PartitionSpec as P

F32 = jnp.float32
BF16 = jnp.bfloat16


def split_parts(values):
    high = values.astype(BF16)
    return high, (values - high.astype(F32)).astype(BF16)


def two_parts(table):
    high = table.astype(BF16)
    low = (table - high.astype(np.float32)).astype(BF16)
    return np.stack([high, low])


def tables(box, window, radix):
    half = window // 2
    coarse = window // radix
    k_all = np.arange(box)
    k_coarse = np.arange(box // radix)
    n_signed = np.arange(window) - half
    low = np.arange(radix)
    y_phase = (radix * np.arange(coarse) - half)[:, None] * low[None, :]
    z_phase = n_signed[:, None] * k_all[None, :]
    right = y_phase[:, None, :, None] + z_phase[None, :, None, :]
    right = right.reshape(coarse * window, radix * box) % box
    x_phase = k_all[:, None] * n_signed[None, :]
    l_phase = radix * k_coarse[:, None] * low[None, :]
    left = l_phase[:, None, :, None] + x_phase[None, :, None, :]
    left = left.reshape(k_coarse.size * box, radix * window) % box
    twist = np.repeat(low[:, None] * low[None, :], box, axis=1) % box

    def pair(phase, scale=1.0):
        angle = phase * (2.0 * math.pi / box)
        return (np.stack([np.cos(angle), np.sin(angle)]) * scale).astype(np.float32)

    right_tab = two_parts(pair(right))
    left_pair = pair(left, 1.0 / box**3)
    left_tab = two_parts(left_pair)
    back_tab = two_parts((left_pair * np.float32(box**3)).transpose(0, 2, 1).copy())
    return right_tab, left_tab, back_tab, pair(twist)


def dot3(lhs, rhs, dims=((1,), (0,))):
    def one(a, b):
        return lax.dot_general(a, b, (dims, ((), ())), preferred_element_type=F32)

    return one(lhs[0], rhs[0]) + (one(lhs[0], rhs[1]) + one(lhs[1], rhs[0]))


def block(cos, sin):
    upper = jnp.concatenate([cos, sin], axis=1)
    lower = jnp.concatenate([-sin, cos], axis=1)
    return jnp.concatenate([upper, lower], axis=0)


def exchange_kernel(
    bands, groups, coef_hbm, rot_ref, pot_hbm, val_ref, pot_out, coef, rots, prod, land,
    coef_sem, rot_send, rot_recv, pot_send, pot_recv, val_send, val_recv, self_sem
):
    band = lax.axis_index("band")
    me = lax.axis_index("ga")
    total = bands * groups
    flat = band * groups + me
    cols = rot_ref.shape[1] // 2
    own = land.shape[1]

    loads = [
        pltpu.make_async_copy(coef_hbm.at[:, c, :], coef.at[c], coef_sem.at[c]) for c in range(2)
    ]
    for load in loads:
        load.start()
    rot_self = pltpu.make_async_copy(rot_ref.at[0], rots.at[me], self_sem.at[0])
    rot_self.start()
    pot_self = pltpu.make_async_copy(pot_hbm, pot_out.at[me], self_sem.at[1])
    pot_self.start()

    barrier = pltpu.get_barrier_semaphore()

    def greet(step, carry):
        to = lax.rem(flat + step, total)
        pl.semaphore_signal(
            barrier, inc=1, device_id={"band": to // groups, "ga": lax.rem(to, groups)},
            device_id_type=pl.DeviceIdType.MESH,
        )
        return carry

    lax.fori_loop(1, total, greet, 0)
    pl.semaphore_wait(barrier, total - 1)

    def rot_copy(to, slot):
        return pltpu.make_async_remote_copy(
            src_ref=rot_ref.at[0], dst_ref=rots.at[slot],
            send_sem=rot_send.at[to], recv_sem=rot_recv.at[slot],
            device_id={"band": band, "ga": to}, device_id_type=pl.DeviceIdType.MESH,
        )

    def pot_copy(to, slot):
        return pltpu.make_async_remote_copy(
            src_ref=pot_hbm, dst_ref=pot_out.at[slot],
            send_sem=pot_send.at[to], recv_sem=pot_recv.at[slot],
            device_id={"band": band, "ga": to}, device_id_type=pl.DeviceIdType.MESH,
        )

    def val_copy(to, slot):
        return pltpu.make_async_remote_copy(
            src_ref=prod.at[pl.ds(to * own, own)], dst_ref=land.at[slot],
            send_sem=val_send.at[to], recv_sem=val_recv.at[slot],
            device_id={"band": to // groups, "ga": lax.rem(to, groups)},
            device_id_type=pl.DeviceIdType.MESH,
        )

    def each(count, mine, act):
        def body(step, carry):
            act(lax.rem(mine + step, count))
            return carry

        lax.fori_loop(1, count, body, 0)

    each(groups, me, lambda to: rot_copy(to, me).start())
    each(groups, me, lambda to: pot_copy(to, me).start())
    for load in loads:
        load.wait()
    rot_self.wait()
    each(groups, me, lambda src: rot_copy(src, src).wait_recv())

    panel = groups * cols
    depth = coef.shape[1]
    real = rots[:, :cols, :].reshape(panel, depth)
    imag = rots[:, cols:, :].reshape(panel, depth)
    high, low = split_parts(jnp.concatenate([real, imag], axis=0))
    both = jnp.concatenate([high, low], axis=0)
    terms = []
    for c in range(2):
        c_high, c_low = split_parts(coef[c])
        first = jnp.dot(both, c_high, preferred_element_type=F32)
        second = jnp.dot(high, c_low, preferred_element_type=F32)
        terms.append(first[: 2 * panel] + (first[2 * panel :] + second))
    prod[:, 0, :] = terms[0][:panel] - terms[1][panel:]
    prod[:, 1, :] = terms[0][panel:] + terms[1][:panel]

    val_self = pltpu.make_async_copy(prod.at[pl.ds(flat * own, own)], land.at[flat], self_sem.at[2])
    val_self.start()
    each(total, flat, lambda to: val_copy(to, flat).start())
    val_self.wait()
    each(total, flat, lambda src: val_copy(src, src).wait_recv())
    summed = land[0:groups]
    for b in range(1, bands):
        summed = summed + land[b * groups : (b + 1) * groups]
    val_ref[...] = summed
    each(total, flat, lambda to: val_copy(to, flat).wait_send())
    each(groups, me, lambda to: rot_copy(to, me).wait_send())
    pot_self.wait()
    each(groups, me, lambda src: pot_copy(src, src).wait_recv())
    each(groups, me, lambda to: pot_copy(to, me).wait_send())


def exchange(coefficients, rotation, potential):
    bands, groups = lax.axis_size("band"), lax.axis_size("ga")
    depth, _, slots = coefficients.shape
    cols = rotation.shape[2]
    panel = cols * groups
    own = panel // (bands * groups)
    rot = rotation.transpose(0, 2, 1).reshape(1, 2 * cols, depth)
    hbm = pl.BlockSpec(memory_space=pl.ANY)
    vmem = pl.BlockSpec(memory_space=pltpu.VMEM)
    dma = pltpu.SemaphoreType.DMA
    return pl.pallas_call(
        functools.partial(exchange_kernel, bands, groups),
        out_shape=(
            jax.ShapeDtypeStruct((groups, own, 2, slots), F32),
            jax.ShapeDtypeStruct((groups,) + potential.shape, F32),
        ),
        in_specs=[hbm, vmem, hbm],
        out_specs=(vmem, hbm),
        scratch_shapes=[
            pltpu.VMEM((2, depth, slots), F32),
            pltpu.VMEM((groups, 2 * cols, depth), F32),
            pltpu.VMEM((panel, 2, slots), F32),
            pltpu.VMEM((bands * groups, own, 2, slots), F32),
            dma((2,)),
            dma((groups,)),
            dma((groups,)),
            dma((groups,)),
            dma((groups,)),
            dma((bands * groups,)),
            dma((bands * groups,)),
            dma((3,)),
        ],
        compiler_params=pltpu.CompilerParams(
            collective_id=0, has_side_effects=True, vmem_limit_bytes=48 * 1024 * 1024
        ),
    )(coefficients, rot, potential)


def apply_kernel(
    box, window, radix, val_ref, row_ref, col_ref, pot_ref, right_ref, left_ref, back_ref, twist_ref, out_ref, acc
):
    coarse = window // radix
    rows = radix * window
    cols = coarse * window
    wide = radix * box
    chunk = val_ref.shape[2]
    acc[...] = jnp.zeros_like(acc)

    def scatter(step, carry):
        at = pl.ds(pl.multiple_of(step * chunk, chunk), chunk)
        row_id = row_ref[:, at]
        col_id = col_ref[:, at]
        picks = lax.broadcasted_iota(jnp.int32, (rows, chunk), 0) == row_id
        onehot = jnp.where(picks, 1.0, 0.0).astype(BF16)
        hits = lax.broadcasted_iota(jnp.int32, (cols, chunk), 0) == col_id
        high, low = split_parts(val_ref[step])
        high, low = high.astype(F32), low.astype(F32)
        placed = [
            jnp.where(hits, part[c : c + 1, :], 0.0).astype(BF16)
            for part in (high, low)
            for c in range(2)
        ]
        acc[...] += lax.dot_general(
            onehot,
            jnp.concatenate(placed, axis=0),
            (((1,), (1,)), ((), ())),
            preferred_element_type=F32,
        )
        return carry

    lax.fori_loop(0, val_ref.shape[0], scatter, 0)
    grid_field = acc[:, : 2 * cols] + acc[:, 2 * cols :]

    right = [block(right_ref[i, 0], right_ref[i, 1]) for i in range(2)]
    field = dot3(split_parts(grid_field), right)
    cos = twist_ref[0][:, None, :]
    sin = twist_ref[1][:, None, :]
    real = field[:, :wide].reshape(radix, window, wide)
    imag = field[:, wide:].reshape(radix, window, wide)
    turned = jnp.concatenate(
        [
            (real * cos - imag * sin).reshape(rows, wide),
            (real * sin + imag * cos).reshape(rows, wide),
        ],
        axis=0,
    )
    left = [block(left_ref[i, 0], -left_ref[i, 1]) for i in range(2)]
    space = dot3(left, split_parts(turned))
    per = pot_ref.shape[0] // (box // radix)
    pot = jnp.concatenate(
        [
            jnp.concatenate([pot_ref[k * per + i] for i in range(per)], axis=1)
            for k in range(box // radix)
        ],
        axis=0,
    )
    space = space * jnp.concatenate([pot, pot], axis=0)
    back = [block(back_ref[i, 0], back_ref[i, 1]) for i in range(2)]
    field = dot3(back, split_parts(space))
    real = field[:rows].reshape(radix, window, wide)
    imag = field[rows:].reshape(radix, window, wide)
    turned = jnp.concatenate(
        [
            (real * cos + imag * sin).reshape(rows, wide),
            (imag * cos - real * sin).reshape(rows, wide),
        ],
        axis=1,
    )
    applied = dot3(split_parts(turned), right, ((1,), (1,)))

    half = window // 2
    row_at = lax.broadcasted_iota(jnp.int32, (rows, cols), 0)
    col_at = lax.broadcasted_iota(jnp.int32, (rows, cols), 1)
    n_x = (row_at % window - half).astype(F32)
    n_y = (col_at // window * radix + row_at // window - half).astype(F32)
    n_z = (col_at % window - half).astype(F32)
    kinetic = (8.0 / (box * box)) * (n_x * n_x + n_y * n_y + n_z * n_z)
    applied = applied + jnp.concatenate([kinetic, kinetic], axis=1) * grid_field
    for c in range(2):
        pieces = [
            applied[lo * window : (lo + 1) * window, c * cols + hi * window : c * cols + (hi + 1) * window]
            for hi in range(coarse)
            for lo in range(radix)
        ]
        out_ref[c] = jnp.concatenate(pieces, axis=1)


def apply_band(values, row_id, col_id, pot_full, window, radix, consts):
    box = pot_full.shape[1]
    vmem = pl.BlockSpec(memory_space=pltpu.VMEM)
    return pl.pallas_call(
        functools.partial(apply_kernel, box, window, radix),
        out_shape=jax.ShapeDtypeStruct((2, window, window * window), F32),
        in_specs=[vmem] * 8,
        out_specs=vmem,
        scratch_shapes=[pltpu.VMEM((radix * window, 4 * (window // radix) * window), F32)],
        compiler_params=pltpu.CompilerParams(vmem_limit_bytes=60 * 1024 * 1024),
    )(values, row_id, col_id, pot_full, *consts)


def per_device(coefficients, rotation, potential, index_map, counts):
    values, pot_full = exchange(coefficients, rotation, potential)
    box = pot_full.shape[1]
    window = box // 2
    half = window // 2
    radix = math.isqrt(box)
    assert radix * radix == box
    slots_each = index_map.shape[0] // counts.shape[0]
    slot_ids = jnp.arange(slots_each, dtype=jnp.int32)
    live = (slot_ids[None, :] < counts[:, None]).reshape(-1)
    cell_x = (index_map // (box * box) + half) % box
    cell_y = (index_map // box % box + half) % box
    cell_z = (index_map % box + half) % box
    inside = (cell_x < window) & (cell_y < window) & (cell_z < window)
    row_id = jnp.where(live & inside, cell_y % radix * window + cell_x, -1)[None]
    col_id = (cell_y // radix * window + cell_z)[None]
    consts = [jnp.asarray(t) for t in tables(box, window, radix)]

    return jnp.stack(
        [
            apply_band(values[:, i], row_id, col_id, pot_full, window, radix, consts)
            for i in range(values.shape[1])
        ]
    )


def solution(mesh):
    placed = (P("band", None, "ga"), P(None, "band", "ga"), P(None, "ga"), P(), P())
    return jax.shard_map(
        per_device,
        mesh=mesh,
        in_specs=placed,
        out_specs=P(("band", "ga"), None, None, None),
        check_vma=False,
    )
```

```python
import functools
import math

import jax
import jax.numpy as jnp
import numpy as np
from jax import lax
from jax.experimental import pallas as pl
from jax.experimental.pallas import tpu as pltpu
from jax.sharding import PartitionSpec as P

F32 = jnp.float32
BF16 = jnp.bfloat16


def split_parts(values):
    high = values.astype(BF16)
    return high, (values - high.astype(F32)).astype(BF16)


def two_parts(table):
    high = table.astype(BF16)
    low = (table - high.astype(np.float32)).astype(BF16)
    return np.stack([high, low])


def tables(box, window, radix):
    half = window // 2
    coarse = window // radix
    k_all = np.arange(box)
    k_coarse = np.arange(box // radix)
    n_signed = np.arange(window) - half
    low = np.arange(radix)
    y_phase = (radix * np.arange(coarse) - half)[:, None] * low[None, :]
    z_phase = n_signed[:, None] * k_all[None, :]
    right = y_phase[:, None, :, None] + z_phase[None, :, None, :]
    right = right.reshape(coarse * window, radix * box) % box
    x_phase = k_all[:, None] * n_signed[None, :]
    l_phase = radix * k_coarse[:, None] * low[None, :]
    left = l_phase[:, None, :, None] + x_phase[None, :, None, :]
    left = left.reshape(k_coarse.size * box, radix * window) % box
    twist = np.repeat(low[:, None] * low[None, :], box, axis=1) % box

    def pair(phase, scale=1.0):
        angle = phase * (2.0 * math.pi / box)
        return (np.stack([np.cos(angle), np.sin(angle)]) * scale).astype(np.float32)

    right_tab = two_parts(pair(right))
    left_pair = pair(left, 1.0 / box**3)
    left_tab = two_parts(left_pair)
    back_tab = two_parts((left_pair * np.float32(box**3)).transpose(0, 2, 1).copy())
    return right_tab, left_tab, back_tab, pair(twist)


def dot3(lhs, rhs, dims=((1,), (0,))):
    def one(a, b):
        return lax.dot_general(a, b, (dims, ((), ())), preferred_element_type=F32)

    return one(lhs[0], rhs[0]) + (one(lhs[0], rhs[1]) + one(lhs[1], rhs[0]))


def block(cos, sin):
    upper = jnp.concatenate([cos, sin], axis=1)
    lower = jnp.concatenate([-sin, cos], axis=1)
    return jnp.concatenate([upper, lower], axis=0)


def exchange_kernel(
    bands, groups, coef_hbm, rot_ref, pot_hbm, val_ref, pot_out, coef, rots, prod, land,
    coef_sem, rot_send, rot_recv, pot_send, pot_recv, pass_send, pass_recv, val_send, val_recv, self_sem
):
    band = lax.axis_index("band")
    me = lax.axis_index("ga")
    total = bands * groups
    flat = band * groups + me
    cols = rot_ref.shape[1] // 2
    own = land.shape[1]
    rows = pot_hbm.shape[0] // bands
    share = pl.ds(pl.multiple_of(band * rows, rows), rows)

    loads = [
        pltpu.make_async_copy(coef_hbm.at[:, c, :], coef.at[c], coef_sem.at[c]) for c in range(2)
    ]
    for load in loads:
        load.start()
    rot_self = pltpu.make_async_copy(rot_ref.at[0], rots.at[me], self_sem.at[0])
    rot_self.start()
    pot_self = pltpu.make_async_copy(pot_hbm, pot_out.at[me], self_sem.at[1])
    pot_self.start()

    barrier = pltpu.get_barrier_semaphore()

    def greet(step, carry):
        to = lax.rem(flat + step, total)
        pl.semaphore_signal(
            barrier, inc=1, device_id={"band": to // groups, "ga": lax.rem(to, groups)},
            device_id_type=pl.DeviceIdType.MESH,
        )
        return carry

    lax.fori_loop(1, total, greet, 0)
    pl.semaphore_wait(barrier, total - 1)

    def rot_copy(to, slot):
        return pltpu.make_async_remote_copy(
            src_ref=rot_ref.at[0], dst_ref=rots.at[slot],
            send_sem=rot_send.at[to], recv_sem=rot_recv.at[slot],
            device_id={"band": band, "ga": to}, device_id_type=pl.DeviceIdType.MESH,
        )

    def pot_copy(to, slot):
        return pltpu.make_async_remote_copy(
            src_ref=pot_hbm.at[share], dst_ref=pot_out.at[slot, share],
            send_sem=pot_send.at[to], recv_sem=pot_recv.at[slot],
            device_id={"band": band, "ga": to}, device_id_type=pl.DeviceIdType.MESH,
        )

    def pass_copy(slot, to, holder):
        held = pl.ds(pl.multiple_of(holder * rows, rows), rows)
        return pltpu.make_async_remote_copy(
            src_ref=pot_out.at[slot, held], dst_ref=pot_out.at[slot, held],
            send_sem=pass_send.at[to, slot], recv_sem=pass_recv.at[holder, slot],
            device_id={"band": to, "ga": me}, device_id_type=pl.DeviceIdType.MESH,
        )

    def val_copy(to, slot):
        return pltpu.make_async_remote_copy(
            src_ref=prod.at[pl.ds(to * own, own)], dst_ref=land.at[slot],
            send_sem=val_send.at[to], recv_sem=val_recv.at[slot],
            device_id={"band": to // groups, "ga": lax.rem(to, groups)},
            device_id_type=pl.DeviceIdType.MESH,
        )

    def each(count, mine, act):
        def body(step, carry):
            act(lax.rem(mine + step, count))
            return carry

        lax.fori_loop(1, count, body, 0)

    each(groups, me, lambda to: rot_copy(to, me).start())
    each(groups, me, lambda to: pot_copy(to, me).start())
    for load in loads:
        load.wait()
    rot_self.wait()
    each(groups, me, lambda src: rot_copy(src, src).wait_recv())

    panel = groups * cols
    depth = coef.shape[1]
    real = rots[:, :cols, :].reshape(panel, depth)
    imag = rots[:, cols:, :].reshape(panel, depth)
    high, low = split_parts(jnp.concatenate([real, imag], axis=0))
    both = jnp.concatenate([high, low], axis=0)
    terms = []
    for c in range(2):
        c_high, c_low = split_parts(coef[c])
        first = jnp.dot(both, c_high, preferred_element_type=F32)
        second = jnp.dot(high, c_low, preferred_element_type=F32)
        terms.append(first[: 2 * panel] + (first[2 * panel :] + second))
    prod[:, 0, :] = terms[0][:panel] - terms[1][panel:]
    prod[:, 1, :] = terms[0][panel:] + terms[1][:panel]

    val_self = pltpu.make_async_copy(prod.at[pl.ds(flat * own, own)], land.at[flat], self_sem.at[2])
    val_self.start()
    each(total, flat, lambda to: val_copy(to, flat).start())

    def relay(src):
        pot_copy(src, src).wait_recv()
        each(bands, band, lambda to: pass_copy(src, to, band).start())

    each(groups, me, relay)
    val_self.wait()
    each(total, flat, lambda src: val_copy(src, src).wait_recv())
    summed = land[0:groups]
    for b in range(1, bands):
        summed = summed + land[b * groups : (b + 1) * groups]
    val_ref[...] = summed
    each(total, flat, lambda to: val_copy(to, flat).wait_send())
    each(groups, me, lambda to: rot_copy(to, me).wait_send())
    pot_self.wait()
    each(groups, me, lambda to: pot_copy(to, me).wait_send())
    each(groups, me, lambda src: each(bands, band, lambda b: pass_copy(src, b, b).wait_recv()))
    each(groups, me, lambda src: each(bands, band, lambda b: pass_copy(src, b, band).wait_send()))


def exchange(coefficients, rotation, potential):
    bands, groups = lax.axis_size("band"), lax.axis_size("ga")
    depth, _, slots = coefficients.shape
    cols = rotation.shape[2]
    panel = cols * groups
    own = panel // (bands * groups)
    rot = rotation.transpose(0, 2, 1).reshape(1, 2 * cols, depth)
    hbm = pl.BlockSpec(memory_space=pl.ANY)
    vmem = pl.BlockSpec(memory_space=pltpu.VMEM)
    dma = pltpu.SemaphoreType.DMA
    return pl.pallas_call(
        functools.partial(exchange_kernel, bands, groups),
        out_shape=(
            jax.ShapeDtypeStruct((groups, own, 2, slots), F32),
            jax.ShapeDtypeStruct((groups,) + potential.shape, F32),
        ),
        in_specs=[hbm, vmem, hbm],
        out_specs=(vmem, hbm),
        scratch_shapes=[
            pltpu.VMEM((2, depth, slots), F32),
            pltpu.VMEM((groups, 2 * cols, depth), F32),
            pltpu.VMEM((panel, 2, slots), F32),
            pltpu.VMEM((bands * groups, own, 2, slots), F32),
            dma((2,)),
            dma((groups,)),
            dma((groups,)),
            dma((groups,)),
            dma((groups,)),
            dma((bands, groups)),
            dma((bands, groups)),
            dma((bands * groups,)),
            dma((bands * groups,)),
            dma((3,)),
        ],
        compiler_params=pltpu.CompilerParams(
            collective_id=0, has_side_effects=True, vmem_limit_bytes=48 * 1024 * 1024
        ),
    )(coefficients, rot, potential)


def apply_kernel(
    box, window, radix, val_ref, row_ref, col_ref, pot_ref, right_ref, left_ref, back_ref, twist_ref, out_ref, acc
):
    coarse = window // radix
    rows = radix * window
    cols = coarse * window
    wide = radix * box
    chunk = val_ref.shape[2]
    acc[...] = jnp.zeros_like(acc)

    def scatter(step, carry):
        at = pl.ds(pl.multiple_of(step * chunk, chunk), chunk)
        row_id = row_ref[:, at]
        col_id = col_ref[:, at]
        picks = lax.broadcasted_iota(jnp.int32, (rows, chunk), 0) == row_id
        onehot = jnp.where(picks, 1.0, 0.0).astype(BF16)
        hits = lax.broadcasted_iota(jnp.int32, (cols, chunk), 0) == col_id
        high, low = split_parts(val_ref[step])
        high, low = high.astype(F32), low.astype(F32)
        placed = [
            jnp.where(hits, part[c : c + 1, :], 0.0).astype(BF16)
            for part in (high, low)
            for c in range(2)
        ]
        acc[...] += lax.dot_general(
            onehot,
            jnp.concatenate(placed, axis=0),
            (((1,), (1,)), ((), ())),
            preferred_element_type=F32,
        )
        return carry

    lax.fori_loop(0, val_ref.shape[0], scatter, 0)
    grid_field = acc[:, : 2 * cols] + acc[:, 2 * cols :]

    right = [block(right_ref[i, 0], right_ref[i, 1]) for i in range(2)]
    field = dot3(split_parts(grid_field), right)
    cos = twist_ref[0][:, None, :]
    sin = twist_ref[1][:, None, :]
    real = field[:, :wide].reshape(radix, window, wide)
    imag = field[:, wide:].reshape(radix, window, wide)
    turned = jnp.concatenate(
        [
            (real * cos - imag * sin).reshape(rows, wide),
            (real * sin + imag * cos).reshape(rows, wide),
        ],
        axis=0,
    )
    left = [block(left_ref[i, 0], -left_ref[i, 1]) for i in range(2)]
    space = dot3(left, split_parts(turned))
    per = pot_ref.shape[0] // (box // radix)
    pot = jnp.concatenate(
        [
            jnp.concatenate([pot_ref[k * per + i] for i in range(per)], axis=1)
            for k in range(box // radix)
        ],
        axis=0,
    )
    space = space * jnp.concatenate([pot, pot], axis=0)
    back = [block(back_ref[i, 0], back_ref[i, 1]) for i in range(2)]
    field = dot3(back, split_parts(space))
    real = field[:rows].reshape(radix, window, wide)
    imag = field[rows:].reshape(radix, window, wide)
    turned = jnp.concatenate(
        [
            (real * cos + imag * sin).reshape(rows, wide),
            (imag * cos - real * sin).reshape(rows, wide),
        ],
        axis=1,
    )
    applied = dot3(split_parts(turned), right, ((1,), (1,)))

    half = window // 2
    row_at = lax.broadcasted_iota(jnp.int32, (rows, cols), 0)
    col_at = lax.broadcasted_iota(jnp.int32, (rows, cols), 1)
    n_x = (row_at % window - half).astype(F32)
    n_y = (col_at // window * radix + row_at // window - half).astype(F32)
    n_z = (col_at % window - half).astype(F32)
    kinetic = (8.0 / (box * box)) * (n_x * n_x + n_y * n_y + n_z * n_z)
    applied = applied + jnp.concatenate([kinetic, kinetic], axis=1) * grid_field
    for c in range(2):
        pieces = [
            applied[lo * window : (lo + 1) * window, c * cols + hi * window : c * cols + (hi + 1) * window]
            for hi in range(coarse)
            for lo in range(radix)
        ]
        out_ref[c] = jnp.concatenate(pieces, axis=1)


def apply_band(values, row_id, col_id, pot_full, window, radix, consts):
    box = pot_full.shape[1]
    vmem = pl.BlockSpec(memory_space=pltpu.VMEM)
    return pl.pallas_call(
        functools.partial(apply_kernel, box, window, radix),
        out_shape=jax.ShapeDtypeStruct((2, window, window * window), F32),
        in_specs=[vmem] * 8,
        out_specs=vmem,
        scratch_shapes=[pltpu.VMEM((radix * window, 4 * (window // radix) * window), F32)],
        compiler_params=pltpu.CompilerParams(vmem_limit_bytes=60 * 1024 * 1024),
    )(values, row_id, col_id, pot_full, *consts)


def per_device(coefficients, rotation, potential, index_map, counts):
    values, pot_full = exchange(coefficients, rotation, potential)
    box = pot_full.shape[1]
    window = box // 2
    half = window // 2
    radix = math.isqrt(box)
    assert radix * radix == box
    slots_each = index_map.shape[0] // counts.shape[0]
    slot_ids = jnp.arange(slots_each, dtype=jnp.int32)
    live = (slot_ids[None, :] < counts[:, None]).reshape(-1)
    cell_x = (index_map // (box * box) + half) % box
    cell_y = (index_map // box % box + half) % box
    cell_z = (index_map % box + half) % box
    inside = (cell_x < window) & (cell_y < window) & (cell_z < window)
    row_id = jnp.where(live & inside, cell_y % radix * window + cell_x, -1)[None]
    col_id = (cell_y // radix * window + cell_z)[None]
    consts = [jnp.asarray(t) for t in tables(box, window, radix)]

    return jnp.stack(
        [
            apply_band(values[:, i], row_id, col_id, pot_full, window, radix, consts)
            for i in range(values.shape[1])
        ]
    )


def solution(mesh):
    placed = (P("band", None, "ga"), P(None, "band", "ga"), P(None, "ga"), P(), P())
    return jax.shard_map(
        per_device,
        mesh=mesh,
        in_specs=placed,
        out_specs=P(("band", "ga"), None, None, None),
        check_vma=False,
    )
```

```python
import functools
import math

import jax
import jax.numpy as jnp
import numpy as np
from jax import lax
from jax.experimental import pallas as pl
from jax.experimental.pallas import tpu as pltpu
from jax.sharding import PartitionSpec as P

F32 = jnp.float32
BF16 = jnp.bfloat16


def split_parts(values):
    high = values.astype(BF16)
    return high, (values - high.astype(F32)).astype(BF16)


def two_parts(table):
    high = table.astype(BF16)
    low = (table - high.astype(np.float32)).astype(BF16)
    return np.stack([high, low])


def tables(box, window, radix):
    half = window // 2
    coarse = window // radix
    k_all = np.arange(box)
    k_coarse = np.arange(box // radix)
    n_signed = np.arange(window) - half
    low = np.arange(radix)
    y_phase = (radix * np.arange(coarse) - half)[:, None] * low[None, :]
    z_phase = n_signed[:, None] * k_all[None, :]
    right = y_phase[:, None, :, None] + z_phase[None, :, None, :]
    right = right.reshape(coarse * window, radix * box) % box
    x_phase = k_all[:, None] * n_signed[None, :]
    l_phase = radix * k_coarse[:, None] * low[None, :]
    left = l_phase[:, None, :, None] + x_phase[None, :, None, :]
    left = left.reshape(k_coarse.size * box, radix * window) % box
    twist = np.repeat(low[:, None] * low[None, :], box, axis=1) % box

    def pair(phase, scale=1.0):
        angle = phase * (2.0 * math.pi / box)
        return (np.stack([np.cos(angle), np.sin(angle)]) * scale).astype(np.float32)

    right_tab = two_parts(pair(right))
    left_pair = pair(left, 1.0 / box**3)
    left_tab = two_parts(left_pair)
    back_tab = two_parts((left_pair * np.float32(box**3)).transpose(0, 2, 1).copy())
    return right_tab, left_tab, back_tab, pair(twist)


def dot3(lhs, rhs, dims=((1,), (0,))):
    def one(a, b):
        return lax.dot_general(a, b, (dims, ((), ())), preferred_element_type=F32)

    return one(lhs[0], rhs[0]) + (one(lhs[0], rhs[1]) + one(lhs[1], rhs[0]))


def block(cos, sin):
    upper = jnp.concatenate([cos, sin], axis=1)
    lower = jnp.concatenate([-sin, cos], axis=1)
    return jnp.concatenate([upper, lower], axis=0)


def whole_kernel(
    bands, groups, box, window, radix, coef_hbm, rot_ref, pot_hbm, row_ref, col_ref,
    right_ref, left_ref, back_ref, twist_ref, out_ref, pot_out, acc, coef, rots, prod, land, vals,
    coef_sem, rot_send, rot_recv, pot_send, pot_recv, pass_send, pass_recv, val_send, val_recv, self_sem
):
    band = lax.axis_index("band")
    me = lax.axis_index("ga")
    total = bands * groups
    flat = band * groups + me
    cols = rot_ref.shape[1] // 2
    own = land.shape[1]
    rows = pot_hbm.shape[0] // bands
    share = pl.ds(pl.multiple_of(band * rows, rows), rows)

    loads = [
        pltpu.make_async_copy(coef_hbm.at[:, c, :], coef.at[c], coef_sem.at[c]) for c in range(2)
    ]
    for load in loads:
        load.start()
    rot_self = pltpu.make_async_copy(rot_ref.at[0], rots.at[me], self_sem.at[0])
    rot_self.start()
    pot_self = pltpu.make_async_copy(pot_hbm, pot_out.at[me], self_sem.at[1])
    pot_self.start()

    barrier = pltpu.get_barrier_semaphore()

    def greet(step, carry):
        to = lax.rem(flat + step, total)
        pl.semaphore_signal(
            barrier, inc=1, device_id={"band": to // groups, "ga": lax.rem(to, groups)},
            device_id_type=pl.DeviceIdType.MESH,
        )
        return carry

    lax.fori_loop(1, total, greet, 0)
    pl.semaphore_wait(barrier, total - 1)

    def rot_copy(to, slot):
        return pltpu.make_async_remote_copy(
            src_ref=rot_ref.at[0], dst_ref=rots.at[slot],
            send_sem=rot_send.at[to], recv_sem=rot_recv.at[slot],
            device_id={"band": band, "ga": to}, device_id_type=pl.DeviceIdType.MESH,
        )

    def pot_copy(to, slot):
        return pltpu.make_async_remote_copy(
            src_ref=pot_hbm.at[share], dst_ref=pot_out.at[slot, share],
            send_sem=pot_send.at[to], recv_sem=pot_recv.at[slot],
            device_id={"band": band, "ga": to}, device_id_type=pl.DeviceIdType.MESH,
        )

    def pass_copy(slot, to, holder):
        held = pl.ds(pl.multiple_of(holder * rows, rows), rows)
        return pltpu.make_async_remote_copy(
            src_ref=pot_out.at[slot, held], dst_ref=pot_out.at[slot, held],
            send_sem=pass_send.at[to, slot], recv_sem=pass_recv.at[holder, slot],
            device_id={"band": to, "ga": me}, device_id_type=pl.DeviceIdType.MESH,
        )

    def val_copy(to, slot):
        return pltpu.make_async_remote_copy(
            src_ref=prod.at[pl.ds(to * own, own)], dst_ref=land.at[slot],
            send_sem=val_send.at[to], recv_sem=val_recv.at[slot],
            device_id={"band": to // groups, "ga": lax.rem(to, groups)},
            device_id_type=pl.DeviceIdType.MESH,
        )

    def each(count, mine, act):
        def body(step, carry):
            act(lax.rem(mine + step, count))
            return carry

        lax.fori_loop(1, count, body, 0)

    each(groups, me, lambda to: rot_copy(to, me).start())
    each(groups, me, lambda to: pot_copy(to, me).start())
    for load in loads:
        load.wait()
    rot_self.wait()
    each(groups, me, lambda src: rot_copy(src, src).wait_recv())

    panel = groups * cols
    depth = coef.shape[1]
    real = rots[:, :cols, :].reshape(panel, depth)
    imag = rots[:, cols:, :].reshape(panel, depth)
    high, low = split_parts(jnp.concatenate([real, imag], axis=0))
    both = jnp.concatenate([high, low], axis=0)
    terms = []
    for c in range(2):
        c_high, c_low = split_parts(coef[c])
        first = jnp.dot(both, c_high, preferred_element_type=F32)
        second = jnp.dot(high, c_low, preferred_element_type=F32)
        terms.append(first[: 2 * panel] + (first[2 * panel :] + second))
    prod[:, 0, :] = terms[0][:panel] - terms[1][panel:]
    prod[:, 1, :] = terms[0][panel:] + terms[1][:panel]

    val_self = pltpu.make_async_copy(prod.at[pl.ds(flat * own, own)], land.at[flat], self_sem.at[2])
    val_self.start()
    each(total, flat, lambda to: val_copy(to, flat).start())

    def relay(src):
        pot_copy(src, src).wait_recv()
        each(bands, band, lambda to: pass_copy(src, to, band).start())

    each(groups, me, relay)
    val_self.wait()
    each(total, flat, lambda src: val_copy(src, src).wait_recv())
    summed = land[0:groups]
    for b in range(1, bands):
        summed = summed + land[b * groups : (b + 1) * groups]
    vals[...] = summed

    def pot_ready():
        pot_self.wait()
        each(groups, me, lambda src: each(bands, band, lambda b: pass_copy(src, b, b).wait_recv()))

    for i in range(own):
        apply_kernel(
            box, window, radix, i, pot_ready if i == 0 else None, vals, row_ref, col_ref, pot_out,
            right_ref, left_ref, back_ref, twist_ref, out_ref, acc
        )
    each(total, flat, lambda to: val_copy(to, flat).wait_send())
    each(groups, me, lambda to: rot_copy(to, me).wait_send())
    each(groups, me, lambda to: pot_copy(to, me).wait_send())
    each(groups, me, lambda src: each(bands, band, lambda b: pass_copy(src, b, band).wait_send()))


def run(coefficients, rotation, potential, row_id, col_id, consts, box, window, radix):
    bands, groups = lax.axis_size("band"), lax.axis_size("ga")
    depth, _, slots = coefficients.shape
    cols = rotation.shape[2]
    panel = cols * groups
    own = panel // (bands * groups)
    rot = rotation.transpose(0, 2, 1).reshape(1, 2 * cols, depth)
    hbm = pl.BlockSpec(memory_space=pl.ANY)
    vmem = pl.BlockSpec(memory_space=pltpu.VMEM)
    dma = pltpu.SemaphoreType.DMA
    return pl.pallas_call(
        functools.partial(whole_kernel, bands, groups, box, window, radix),
        out_shape=jax.ShapeDtypeStruct((own, 2, window, window * window), F32),
        in_specs=[hbm, vmem, hbm] + [vmem] * 6,
        out_specs=vmem,
        scratch_shapes=[
            pltpu.VMEM((groups,) + potential.shape, F32),
            pltpu.VMEM((radix * window, 4 * (window // radix) * window), F32),
            pltpu.VMEM((2, depth, slots), F32),
            pltpu.VMEM((groups, 2 * cols, depth), F32),
            pltpu.VMEM((panel, 2, slots), F32),
            pltpu.VMEM((bands * groups, own, 2, slots), F32),
            pltpu.VMEM((groups, own, 2, slots), F32),
            dma((2,)),
            dma((groups,)),
            dma((groups,)),
            dma((groups,)),
            dma((groups,)),
            dma((bands, groups)),
            dma((bands, groups)),
            dma((bands * groups,)),
            dma((bands * groups,)),
            dma((3,)),
        ],
        compiler_params=pltpu.CompilerParams(
            collective_id=0, has_side_effects=True, vmem_limit_bytes=60 * 1024 * 1024
        ),
    )(coefficients, rot, potential, row_id, col_id, *consts)


def apply_kernel(
    box, window, radix, index, pot_ready, val_ref, row_ref, col_ref, pot_ref, right_ref, left_ref, back_ref, twist_ref, out_ref, acc
):
    coarse = window // radix
    rows = radix * window
    cols = coarse * window
    wide = radix * box
    chunk = val_ref.shape[3]
    acc[...] = jnp.zeros_like(acc)

    def scatter(step, carry):
        at = pl.ds(pl.multiple_of(step * chunk, chunk), chunk)
        row_id = row_ref[:, at]
        col_id = col_ref[:, at]
        picks = lax.broadcasted_iota(jnp.int32, (rows, chunk), 0) == row_id
        onehot = jnp.where(picks, 1.0, 0.0).astype(BF16)
        hits = lax.broadcasted_iota(jnp.int32, (cols, chunk), 0) == col_id
        high, low = split_parts(val_ref[step, index])
        high, low = high.astype(F32), low.astype(F32)
        placed = [
            jnp.where(hits, part[c : c + 1, :], 0.0).astype(BF16)
            for part in (high, low)
            for c in range(2)
        ]
        acc[...] += lax.dot_general(
            onehot,
            jnp.concatenate(placed, axis=0),
            (((1,), (1,)), ((), ())),
            preferred_element_type=F32,
        )
        return carry

    lax.fori_loop(0, val_ref.shape[0], scatter, 0)
    grid_field = acc[:, : 2 * cols] + acc[:, 2 * cols :]

    right = [block(right_ref[i, 0], right_ref[i, 1]) for i in range(2)]
    field = dot3(split_parts(grid_field), right)
    cos = twist_ref[0][:, None, :]
    sin = twist_ref[1][:, None, :]
    real = field[:, :wide].reshape(radix, window, wide)
    imag = field[:, wide:].reshape(radix, window, wide)
    turned = jnp.concatenate(
        [
            (real * cos - imag * sin).reshape(rows, wide),
            (real * sin + imag * cos).reshape(rows, wide),
        ],
        axis=0,
    )
    left = [block(left_ref[i, 0], -left_ref[i, 1]) for i in range(2)]
    space = dot3(left, split_parts(turned))
    if pot_ready is not None:
        pot_ready()
    per = pot_ref.shape[0] // (box // radix)
    pot = jnp.concatenate(
        [
            jnp.concatenate([pot_ref[k * per + i] for i in range(per)], axis=1)
            for k in range(box // radix)
        ],
        axis=0,
    )
    space = space * jnp.concatenate([pot, pot], axis=0)
    back = [block(back_ref[i, 0], back_ref[i, 1]) for i in range(2)]
    field = dot3(back, split_parts(space))
    real = field[:rows].reshape(radix, window, wide)
    imag = field[rows:].reshape(radix, window, wide)
    turned = jnp.concatenate(
        [
            (real * cos + imag * sin).reshape(rows, wide),
            (imag * cos - real * sin).reshape(rows, wide),
        ],
        axis=1,
    )
    applied = dot3(split_parts(turned), right, ((1,), (1,)))

    half = window // 2
    row_at = lax.broadcasted_iota(jnp.int32, (rows, cols), 0)
    col_at = lax.broadcasted_iota(jnp.int32, (rows, cols), 1)
    n_x = (row_at % window - half).astype(F32)
    n_y = (col_at // window * radix + row_at // window - half).astype(F32)
    n_z = (col_at % window - half).astype(F32)
    kinetic = (8.0 / (box * box)) * (n_x * n_x + n_y * n_y + n_z * n_z)
    applied = applied + jnp.concatenate([kinetic, kinetic], axis=1) * grid_field
    for c in range(2):
        pieces = [
            applied[lo * window : (lo + 1) * window, c * cols + hi * window : c * cols + (hi + 1) * window]
            for hi in range(coarse)
            for lo in range(radix)
        ]
        out_ref[index, c] = jnp.concatenate(pieces, axis=1)


def per_device(coefficients, rotation, potential, index_map, counts):
    box = potential.shape[0]
    window = box // 2
    half = window // 2
    radix = math.isqrt(box)
    assert radix * radix == box
    slots_each = index_map.shape[0] // counts.shape[0]
    slot_ids = jnp.arange(slots_each, dtype=jnp.int32)
    live = (slot_ids[None, :] < counts[:, None]).reshape(-1)
    cell_x = (index_map // (box * box) + half) % box
    cell_y = (index_map // box % box + half) % box
    cell_z = (index_map % box + half) % box
    inside = (cell_x < window) & (cell_y < window) & (cell_z < window)
    row_id = jnp.where(live & inside, cell_y % radix * window + cell_x, -1)[None]
    col_id = (cell_y // radix * window + cell_z)[None]
    consts = [jnp.asarray(t) for t in tables(box, window, radix)]

    return run(coefficients, rotation, potential, row_id, col_id, consts, box, window, radix)


def solution(mesh):
    placed = (P("band", None, "ga"), P(None, "band", "ga"), P(None, "ga"), P(), P())
    return jax.shard_map(
        per_device,
        mesh=mesh,
        in_specs=placed,
        out_specs=P(("band", "ga"), None, None, None),
        check_vma=False,
    )
```

```python
import functools
import math

import jax
import jax.numpy as jnp
import numpy as np
from jax import lax
from jax.experimental import pallas as pl
from jax.experimental.pallas import tpu as pltpu
from jax.sharding import PartitionSpec as P

F32 = jnp.float32
BF16 = jnp.bfloat16


def split_parts(values):
    high = values.astype(BF16)
    return high, (values - high.astype(F32)).astype(BF16)


def two_parts(table):
    high = table.astype(BF16)
    low = (table - high.astype(np.float32)).astype(BF16)
    return np.stack([high, low])


def tables(box, window, radix):
    half = window // 2
    coarse = window // radix
    k_all = np.arange(box)
    k_coarse = np.arange(box // radix)
    n_signed = np.arange(window) - half
    low = np.arange(radix)
    y_phase = (radix * np.arange(coarse) - half)[:, None] * low[None, :]
    z_phase = n_signed[:, None] * k_all[None, :]
    right = y_phase[:, None, :, None] + z_phase[None, :, None, :]
    right = right.reshape(coarse * window, radix * box) % box
    x_phase = k_all[:, None] * n_signed[None, :]
    l_phase = radix * k_coarse[:, None] * low[None, :]
    left = l_phase[:, None, :, None] + x_phase[None, :, None, :]
    left = left.reshape(k_coarse.size * box, radix * window) % box
    twist = np.repeat(low[:, None] * low[None, :], box, axis=1) % box

    def pair(phase, scale=1.0):
        angle = phase * (2.0 * math.pi / box)
        return (np.stack([np.cos(angle), np.sin(angle)]) * scale).astype(np.float32)

    right_tab = two_parts(pair(right))
    left_pair = pair(left, 1.0 / box**3)
    left_tab = two_parts(left_pair)
    back_tab = two_parts((left_pair * np.float32(box**3)).transpose(0, 2, 1).copy())
    return right_tab, left_tab, back_tab, pair(twist)


def dot3(lhs, rhs, dims=((1,), (0,))):
    def one(a, b):
        return lax.dot_general(a, b, (dims, ((), ())), preferred_element_type=F32)

    return one(lhs[0], rhs[0]) + (one(lhs[0], rhs[1]) + one(lhs[1], rhs[0]))


def block(cos, sin):
    upper = jnp.concatenate([cos, sin], axis=1)
    lower = jnp.concatenate([-sin, cos], axis=1)
    return jnp.concatenate([upper, lower], axis=0)


def whole_kernel(
    bands, groups, box, window, radix, coef_hbm, rot_ref, pot_hbm, row_ref, col_ref,
    right_hbm, left_hbm, back_hbm, twist_ref, out_ref, right_ref, left_ref, back_ref, tab_sem, pot_out, acc, coef, rots, prod, land, vals,
    coef_sem, rot_send, rot_recv, pot_send, pot_recv, pass_send, pass_recv, val_send, val_recv, self_sem
):
    band = lax.axis_index("band")
    me = lax.axis_index("ga")
    total = bands * groups
    flat = band * groups + me
    cols = rot_ref.shape[1] // 2
    own = land.shape[1]
    rows = pot_hbm.shape[0] // bands
    share = pl.ds(pl.multiple_of(band * rows, rows), rows)

    loads = [
        pltpu.make_async_copy(coef_hbm.at[:, c, :], coef.at[c], coef_sem.at[c]) for c in range(2)
    ]
    for load in loads:
        load.start()
    tabs = [
        pltpu.make_async_copy(src, dst, tab_sem.at[i])
        for i, (src, dst) in enumerate(
            ((right_hbm, right_ref), (left_hbm, left_ref), (back_hbm, back_ref))
        )
    ]
    for tab in tabs:
        tab.start()
    rot_self = pltpu.make_async_copy(rot_ref.at[0], rots.at[me], self_sem.at[0])
    rot_self.start()
    pot_self = pltpu.make_async_copy(pot_hbm, pot_out.at[me], self_sem.at[1])
    pot_self.start()

    barrier = pltpu.get_barrier_semaphore()

    def greet(step, carry):
        to = lax.rem(flat + step, total)
        pl.semaphore_signal(
            barrier, inc=1, device_id={"band": to // groups, "ga": lax.rem(to, groups)},
            device_id_type=pl.DeviceIdType.MESH,
        )
        return carry

    lax.fori_loop(1, total, greet, 0)
    pl.semaphore_wait(barrier, total - 1)

    def rot_copy(to, slot):
        return pltpu.make_async_remote_copy(
            src_ref=rot_ref.at[0], dst_ref=rots.at[slot],
            send_sem=rot_send.at[to], recv_sem=rot_recv.at[slot],
            device_id={"band": band, "ga": to}, device_id_type=pl.DeviceIdType.MESH,
        )

    def pot_copy(to, slot):
        return pltpu.make_async_remote_copy(
            src_ref=pot_hbm.at[share], dst_ref=pot_out.at[slot, share],
            send_sem=pot_send.at[to], recv_sem=pot_recv.at[slot],
            device_id={"band": band, "ga": to}, device_id_type=pl.DeviceIdType.MESH,
        )

    def pass_copy(slot, to, holder):
        held = pl.ds(pl.multiple_of(holder * rows, rows), rows)
        return pltpu.make_async_remote_copy(
            src_ref=pot_out.at[slot, held], dst_ref=pot_out.at[slot, held],
            send_sem=pass_send.at[to, slot], recv_sem=pass_recv.at[holder, slot],
            device_id={"band": to, "ga": me}, device_id_type=pl.DeviceIdType.MESH,
        )

    def val_copy(to, slot):
        return pltpu.make_async_remote_copy(
            src_ref=prod.at[pl.ds(to * own, own)], dst_ref=land.at[slot],
            send_sem=val_send.at[to], recv_sem=val_recv.at[slot],
            device_id={"band": to // groups, "ga": lax.rem(to, groups)},
            device_id_type=pl.DeviceIdType.MESH,
        )

    def each(count, mine, act):
        def body(step, carry):
            act(lax.rem(mine + step, count))
            return carry

        lax.fori_loop(1, count, body, 0)

    each(groups, me, lambda to: rot_copy(to, me).start())
    each(groups, me, lambda to: pot_copy(to, me).start())
    for load in loads:
        load.wait()
    rot_self.wait()
    each(groups, me, lambda src: rot_copy(src, src).wait_recv())

    panel = groups * cols
    depth = coef.shape[1]
    real = rots[:, :cols, :].reshape(panel, depth)
    imag = rots[:, cols:, :].reshape(panel, depth)
    high, low = split_parts(jnp.concatenate([real, imag], axis=0))
    both = jnp.concatenate([high, low], axis=0)
    terms = []
    for c in range(2):
        c_high, c_low = split_parts(coef[c])
        first = jnp.dot(both, c_high, preferred_element_type=F32)
        second = jnp.dot(high, c_low, preferred_element_type=F32)
        terms.append(first[: 2 * panel] + (first[2 * panel :] + second))
    prod[:, 0, :] = terms[0][:panel] - terms[1][panel:]
    prod[:, 1, :] = terms[0][panel:] + terms[1][:panel]

    val_self = pltpu.make_async_copy(prod.at[pl.ds(flat * own, own)], land.at[flat], self_sem.at[2])
    val_self.start()
    each(total, flat, lambda to: val_copy(to, flat).start())

    def relay(src):
        pot_copy(src, src).wait_recv()
        each(bands, band, lambda to: pass_copy(src, to, band).start())

    each(groups, me, relay)
    val_self.wait()
    each(total, flat, lambda src: val_copy(src, src).wait_recv())
    summed = land[0:groups]
    for b in range(1, bands):
        summed = summed + land[b * groups : (b + 1) * groups]
    vals[...] = summed
    for tab in tabs:
        tab.wait()

    def pot_ready():
        pot_self.wait()
        each(groups, me, lambda src: each(bands, band, lambda b: pass_copy(src, b, b).wait_recv()))

    for i in range(own):
        apply_kernel(
            box, window, radix, i, pot_ready if i == 0 else None, vals, row_ref, col_ref, pot_out,
            right_ref, left_ref, back_ref, twist_ref, out_ref, acc
        )
    each(total, flat, lambda to: val_copy(to, flat).wait_send())
    each(groups, me, lambda to: rot_copy(to, me).wait_send())
    each(groups, me, lambda to: pot_copy(to, me).wait_send())
    each(groups, me, lambda src: each(bands, band, lambda b: pass_copy(src, b, band).wait_send()))


def run(coefficients, rotation, potential, row_id, col_id, consts, box, window, radix):
    bands, groups = lax.axis_size("band"), lax.axis_size("ga")
    depth, _, slots = coefficients.shape
    cols = rotation.shape[2]
    panel = cols * groups
    own = panel // (bands * groups)
    rot = rotation.transpose(0, 2, 1).reshape(1, 2 * cols, depth)
    hbm = pl.BlockSpec(memory_space=pl.ANY)
    vmem = pl.BlockSpec(memory_space=pltpu.VMEM)
    dma = pltpu.SemaphoreType.DMA
    return pl.pallas_call(
        functools.partial(whole_kernel, bands, groups, box, window, radix),
        out_shape=jax.ShapeDtypeStruct((own, 2, window, window * window), F32),
        in_specs=[hbm, vmem, hbm] + [vmem] * 2 + [hbm] * 3 + [vmem],
        out_specs=vmem,
        scratch_shapes=[
            *[pltpu.VMEM(table.shape, table.dtype) for table in consts[:3]],
            dma((3,)),
            pltpu.VMEM((groups,) + potential.shape, F32),
            pltpu.VMEM((radix * window, 4 * (window // radix) * window), F32),
            pltpu.VMEM((2, depth, slots), F32),
            pltpu.VMEM((groups, 2 * cols, depth), F32),
            pltpu.VMEM((panel, 2, slots), F32),
            pltpu.VMEM((bands * groups, own, 2, slots), F32),
            pltpu.VMEM((groups, own, 2, slots), F32),
            dma((2,)),
            dma((groups,)),
            dma((groups,)),
            dma((groups,)),
            dma((groups,)),
            dma((bands, groups)),
            dma((bands, groups)),
            dma((bands * groups,)),
            dma((bands * groups,)),
            dma((3,)),
        ],
        compiler_params=pltpu.CompilerParams(
            collective_id=0, has_side_effects=True, vmem_limit_bytes=60 * 1024 * 1024
        ),
    )(coefficients, rot, potential, row_id, col_id, *consts)


def apply_kernel(
    box, window, radix, index, pot_ready, val_ref, row_ref, col_ref, pot_ref, right_ref, left_ref, back_ref, twist_ref, out_ref, acc
):
    coarse = window // radix
    rows = radix * window
    cols = coarse * window
    wide = radix * box
    chunk = val_ref.shape[3]
    acc[...] = jnp.zeros_like(acc)

    def scatter(step, carry):
        at = pl.ds(pl.multiple_of(step * chunk, chunk), chunk)
        row_id = row_ref[:, at]
        col_id = col_ref[:, at]
        picks = lax.broadcasted_iota(jnp.int32, (rows, chunk), 0) == row_id
        onehot = jnp.where(picks, 1.0, 0.0).astype(BF16)
        hits = lax.broadcasted_iota(jnp.int32, (cols, chunk), 0) == col_id
        high, low = split_parts(val_ref[step, index])
        high, low = high.astype(F32), low.astype(F32)
        placed = [
            jnp.where(hits, part[c : c + 1, :], 0.0).astype(BF16)
            for part in (high, low)
            for c in range(2)
        ]
        acc[...] += lax.dot_general(
            onehot,
            jnp.concatenate(placed, axis=0),
            (((1,), (1,)), ((), ())),
            preferred_element_type=F32,
        )
        return carry

    lax.fori_loop(0, val_ref.shape[0], scatter, 0)
    grid_field = acc[:, : 2 * cols] + acc[:, 2 * cols :]

    right = [block(right_ref[i, 0], right_ref[i, 1]) for i in range(2)]
    field = dot3(split_parts(grid_field), right)
    cos = twist_ref[0][:, None, :]
    sin = twist_ref[1][:, None, :]
    real = field[:, :wide].reshape(radix, window, wide)
    imag = field[:, wide:].reshape(radix, window, wide)
    turned = jnp.concatenate(
        [
            (real * cos - imag * sin).reshape(rows, wide),
            (real * sin + imag * cos).reshape(rows, wide),
        ],
        axis=0,
    )
    left = [block(left_ref[i, 0], -left_ref[i, 1]) for i in range(2)]
    space = dot3(left, split_parts(turned))
    if pot_ready is not None:
        pot_ready()
    per = pot_ref.shape[0] // (box // radix)
    pot = jnp.concatenate(
        [
            jnp.concatenate([pot_ref[k * per + i] for i in range(per)], axis=1)
            for k in range(box // radix)
        ],
        axis=0,
    )
    space = space * jnp.concatenate([pot, pot], axis=0)
    back = [block(back_ref[i, 0], back_ref[i, 1]) for i in range(2)]
    field = dot3(back, split_parts(space))
    real = field[:rows].reshape(radix, window, wide)
    imag = field[rows:].reshape(radix, window, wide)
    turned = jnp.concatenate(
        [
            (real * cos + imag * sin).reshape(rows, wide),
            (imag * cos - real * sin).reshape(rows, wide),
        ],
        axis=1,
    )
    applied = dot3(split_parts(turned), right, ((1,), (1,)))

    half = window // 2
    row_at = lax.broadcasted_iota(jnp.int32, (rows, cols), 0)
    col_at = lax.broadcasted_iota(jnp.int32, (rows, cols), 1)
    n_x = (row_at % window - half).astype(F32)
    n_y = (col_at // window * radix + row_at // window - half).astype(F32)
    n_z = (col_at % window - half).astype(F32)
    kinetic = (8.0 / (box * box)) * (n_x * n_x + n_y * n_y + n_z * n_z)
    applied = applied + jnp.concatenate([kinetic, kinetic], axis=1) * grid_field
    for c in range(2):
        pieces = [
            applied[lo * window : (lo + 1) * window, c * cols + hi * window : c * cols + (hi + 1) * window]
            for hi in range(coarse)
            for lo in range(radix)
        ]
        out_ref[index, c] = jnp.concatenate(pieces, axis=1)


def per_device(coefficients, rotation, potential, index_map, counts):
    box = potential.shape[0]
    window = box // 2
    half = window // 2
    radix = math.isqrt(box)
    assert radix * radix == box
    slots_each = index_map.shape[0] // counts.shape[0]
    slot_ids = jnp.arange(slots_each, dtype=jnp.int32)
    live = (slot_ids[None, :] < counts[:, None]).reshape(-1)
    cell_x = (index_map // (box * box) + half) % box
    cell_y = (index_map // box % box + half) % box
    cell_z = (index_map % box + half) % box
    inside = (cell_x < window) & (cell_y < window) & (cell_z < window)
    row_id = jnp.where(live & inside, cell_y % radix * window + cell_x, -1)[None]
    col_id = (cell_y // radix * window + cell_z)[None]
    consts = [jnp.asarray(t) for t in tables(box, window, radix)]

    return run(coefficients, rotation, potential, row_id, col_id, consts, box, window, radix)


def solution(mesh):
    placed = (P("band", None, "ga"), P(None, "band", "ga"), P(None, "ga"), P(), P())
    return jax.shard_map(
        per_device,
        mesh=mesh,
        in_specs=placed,
        out_specs=P(("band", "ga"), None, None, None),
        check_vma=False,
    )
```
